32 devices in a mesh: seq: 8 (over z, x), tensor: 4 (over y, core).
Axes of the slice: x: 2, y: 2, z: 4, core: 2. Of those that a mesh axis runs over, the one named last changes fastest.
Arguments:
- queries: bfloat16 [8192, 8192], P('seq', 'tensor'), may hold values from -6 to 6
- keys: bfloat16 [8192, 1024], P('seq', 'tensor'), may hold values from -6 to 6
- values: bfloat16 [8192, 1024], P('seq', 'tensor'), may hold values from -6 to 6
- key_blocks: int32 [64, 64, 16], P('tensor'), may hold values from 0 to 63, as said below
- block_counts: int32 [64, 64], P('tensor'), may hold values from 1 to 16, as said below
- out_weight: bfloat16 [8192, 8192], P('tensor'), may hold values from -0.59765625 to 0.59765625
Outputs:
- projected: bfloat16 [8192, 8192], P('seq', 'tensor')
The draws below stay inside these ranges and needn't reach their ends.
Inputs may be any that keep to these rules, and one draw needn't show every extreme that they name: For head h and query block b the first block_counts[h, b] entries of key_blocks[h, b] are different blocks of 0 to b, the first being b itself; the later entries are block numbers without meaning. block_counts[h, b] is at most b + 1; the last query block of every head has exactly 16.
All inputs are finite; a program needn't handle non-finite values.
Results may differ from the reference program's by a relative error of at most 0.014.
Values may be sent and summed in bfloat16 or wider, within the bound.
A program may use at most 128 MiB of HBM per device.

```python
import jax
import jax.numpy as jnp
from jax import lax

D = 8192
HEADS = 64
KV_HEADS = 8
HEAD_DIM = 128
BLOCK = 128
KMAX = 16
SEQ = 8192
NB = 64
HQ_DEV = 16
N_TENSOR = 4


def draw_queries(key, part):
    base = jnp.clip(jax.random.normal(jax.random.fold_in(key, 1), (SEQ, HEADS * HEAD_DIM), jnp.float32), -6.0, 6.0)
    return base.astype(jnp.bfloat16)


def draw_keys(key, part):
    base = jnp.clip(jax.random.normal(jax.random.fold_in(key, 3), (SEQ, KV_HEADS * HEAD_DIM), jnp.float32), -6.0, 6.0)
    return base.astype(jnp.bfloat16)


def mask_layout(key):
    base = jax.random.fold_in(key, 29)
    rows = jnp.arange(NB, dtype=jnp.int32)
    density = jax.random.randint(jax.random.fold_in(base, 1), (HEADS, 1), 1, 5)
    cap = 1 + (KMAX - 1) * (rows[None, :] + 1) * density // (NB * 4)
    low = jnp.maximum(1, cap // 2)
    counts = jax.random.randint(jax.random.fold_in(base, 2), (HEADS, NB), low, cap + 1)
    counts = jnp.minimum(counts, rows[None, :] + 1)
    counts = jnp.where(rows[None, :] == NB - 1, KMAX, counts).astype(jnp.int32)
    kind = jax.random.randint(jax.random.fold_in(base, 3), (HEADS, 1, 1), 0, 2)
    vertical = jax.random.randint(jax.random.fold_in(base, 4), (HEADS, 1, NB), 0, 4) == 0
    slash_set = jax.random.randint(jax.random.fold_in(base, 5), (HEADS, NB), 0, 4) == 0
    slash_set = slash_set | (rows[None, :] == 1)
    offsets = jnp.mod(rows[:, None] - rows[None, :], NB)
    slash_hit = slash_set[:, offsets]
    scattered = jax.random.randint(jax.random.fold_in(base, 6), (HEADS, NB, NB), 0, 3) == 0
    noise = jax.random.randint(jax.random.fold_in(base, 7), (HEADS, NB, NB), 0, 1000)
    pattern = jnp.where(kind == 0, 2000 * vertical.astype(jnp.int32) + 2000 * slash_hit.astype(jnp.int32), 2000 * scattered.astype(jnp.int32))
    valid = (rows[None, None, :] <= rows[None, :, None]).astype(jnp.int32)
    diagonal = (rows[None, None, :] == rows[None, :, None]).astype(jnp.int32)
    score = valid * (200000 + noise + pattern) + diagonal * 200000
    distinct = score * NB + rows[None, None, :]
    slots = lax.top_k(distinct, KMAX)[1].astype(jnp.int32)
    return (slots, counts)


def draw_key_blocks(key, part):
    return mask_layout(key)[0]


def draw_block_counts(key, part):
    return mask_layout(key)[1]


def with_spikes(entries, key, source, target, blocks, factor):
    def block_of(position):
        return (jnp.arange(entries.shape[position]) // (entries.shape[position] // blocks)).reshape((-1,) + (1,) * (entries.ndim - 1 - position))

    one_side = jax.random.permutation(key, blocks)[block_of(target)]
    second = (block_of(target) + blocks // 2) % blocks
    return jnp.where((block_of(source) == one_side) | (block_of(source) == second), factor * entries, entries)


def block_scale(own_key, dims, split, smallest, high):
    loudness = 1.0
    for dim, blocks in split:
        heights = jax.random.uniform(jax.random.fold_in(jax.random.fold_in(own_key, 6), dim), (blocks,), jnp.float32, smallest / len(split), high / len(split))
        loudness = loudness * jnp.repeat(jnp.exp(heights), dims[dim] // blocks).reshape((-1,) + (1,) * (len(dims) - 1 - dim))
    return loudness


def centred(own_key, shape, deviation, bound, split=(), kind=jnp.bfloat16):
    factor_of = block_scale(own_key, shape, split, -0.22, 0.18) if split else 1.0
    result = jax.random.normal(own_key, shape, jnp.float32) * deviation * factor_of
    return jnp.minimum(jnp.maximum(result, -bound), bound).astype(kind)


def noise_with(own_key, dims, deviation, limit, pieces, heavy, held_as=jnp.bfloat16):
    array = deviation * jax.random.normal(own_key, dims, jnp.float32)
    if pieces:
        array = array * block_scale(own_key, dims, pieces, -0.22, 0.18)
    return jnp.clip(with_spikes(array, jax.random.fold_in(own_key, 3), *heavy), -limit, limit).astype(held_as)


def setup_inputs(seed: int = 0) -> dict:
    splits = jax.random.split(jax.random.key(seed), 7)
    queries = draw_queries(jax.random.fold_in(splits[6], 71), 0)
    keys = draw_keys(jax.random.fold_in(splits[6], 71), 0)
    values = centred(splits[2], (SEQ, KV_HEADS * HEAD_DIM), 1.0, 6.0, ((0, 8), (1, 4)))
    key_blocks = draw_key_blocks(jax.random.fold_in(splits[6], 71), 0)
    block_counts = draw_block_counts(jax.random.fold_in(splits[6], 71), 0)
    out_weight = noise_with(splits[5], (HEADS * HEAD_DIM, D), 0.1, 0.59765625, ((0, 4),), (0, 1, 4, 2.0))
    return {"queries": queries, "keys": keys, "values": values, "key_blocks": key_blocks, "block_counts": block_counts, "out_weight": out_weight}


neg_large = -1.0e30


def reference(queries, keys, values, key_blocks, block_counts, out_weight):
    seq_len = queries.shape[0]
    nblocks = seq_len // BLOCK
    ratio = HEADS // KV_HEADS
    softmax_scale = HEAD_DIM ** -0.5
    q_all = queries.reshape(nblocks, BLOCK, HEADS, HEAD_DIM)
    k_all = keys.reshape(nblocks, BLOCK, KV_HEADS, HEAD_DIM)
    v_all = values.reshape(nblocks, BLOCK, KV_HEADS, HEAD_DIM)
    q_pos = jnp.arange(BLOCK, dtype=jnp.int32)[:, None]
    k_pos = jnp.arange(BLOCK, dtype=jnp.int32)[None, :]
    block_ids = jnp.arange(nblocks, dtype=jnp.int32)
    slot_ids = jnp.arange(KMAX, dtype=jnp.int32)

    def one_head(head):
        group = head // ratio
        query_per_head = lax.dynamic_index_in_dim(q_all, head, 2, keepdims=False).astype(jnp.float32)
        k_head = lax.dynamic_index_in_dim(k_all, group, 2, keepdims=False).astype(jnp.float32)
        v_head = lax.dynamic_index_in_dim(v_all, group, 2, keepdims=False).astype(jnp.float32)
        slots = lax.dynamic_index_in_dim(key_blocks, head, 0, keepdims=False)
        counts = lax.dynamic_index_in_dim(block_counts, head, 0, keepdims=False)
        selected_key_rows = k_head[slots]
        selected_value_rows = v_head[slots]
        logit_scores = jnp.einsum("imh,itzh->imtz", query_per_head, selected_key_rows) * softmax_scale
        slot_used = slot_ids[None, :] < counts[:, None]
        earlier = slots < block_ids[:, None]
        visible = slot_used[:, None, :, None] & (earlier[:, None, :, None] | (q_pos >= k_pos)[None, :, None, :])
        masked = jnp.where(visible, logit_scores, neg_large)
        top = jnp.max(masked, axis=(2, 3))
        weights = jnp.where(visible, jnp.exp(masked - top[:, :, None, None]), 0.0)
        total = jnp.sum(weights, axis=(2, 3))
        rounded_output = lax.optimization_barrier(weights.astype(jnp.bfloat16)).astype(jnp.float32)
        summed_heads = jnp.einsum("xuin,xinw->xuw", rounded_output, selected_value_rows)
        return (summed_heads / total[:, :, None]).astype(jnp.bfloat16)

    attended = lax.map(one_head, jnp.arange(HEADS, dtype=jnp.int32))
    attended = attended.transpose(1, 2, 0, 3).reshape(seq_len, HEADS * HEAD_DIM)
    width = HQ_DEV * HEAD_DIM
    groups = attended.reshape(seq_len, N_TENSOR, width).transpose(1, 0, 2)
    weight_groups = out_weight.reshape(N_TENSOR, width, D)

    def add_group(total, pair):
        part = jnp.dot(pair[0], pair[1], preferred_element_type=jnp.float32)
        part = lax.optimization_barrier(part.astype(jnp.bfloat16)).astype(jnp.float32)
        return total + part, None

    summed_heads, _ = lax.scan(add_group, jnp.zeros((seq_len, D), jnp.float32), (groups, weight_groups))
    return summed_heads.astype(jnp.bfloat16)
```

```python
import functools

import jax
import jax.numpy as jnp
from jax import lax
from jax.experimental import pallas as pl
from jax.experimental.pallas import tpu as pltpu
from jax.sharding import PartitionSpec as P


HEAD_DIM = 128
BLOCK = 128
LOG2E = 1.4426950408889634
NEG = -1e30
PAIR = 2
DEPTHS = (2, 4, 6, 8, 12)
PIECES = 8
EARLY = 4
LATE = 4
VMEM = 62 << 20
MESH = pl.DeviceIdType.MESH


def gather_kernel(*refs, along, across, width, groups, kvs):
    owns, w_ref = refs[:kvs], refs[kvs]
    buf_ref, w2_ref = refs[kvs + 1], refs[kvs + 2]
    n_ahead = across if kvs > 1 else 0
    ahead = refs[kvs + 3 : kvs + 3 + n_ahead]
    zs, zr, xs, xr, rs, rr, ws, wr, hs, hr = refs[kvs + 3 + n_ahead :]
    own_ref = owns[0]
    seq = lax.axis_index("seq")
    z = seq // across
    x = lax.rem(seq, across)
    up = lax.rem(z + 1, along) * across + x
    down = lax.rem(z + along - 1, along) * across + x
    sides = [z * across + lax.rem(x + m, across) for m in range(1, across)]
    core = lax.rem(lax.axis_index("tensor"), 2)
    partner = lax.axis_index("tensor") + 1 - 2 * core
    barrier = pltpu.get_barrier_semaphore()
    for other in [up, down] + sides:
        pl.semaphore_signal(barrier, inc=1, device_id={"seq": other}, device_id_type=MESH)
    pl.semaphore_signal(barrier, inc=1, device_id={"tensor": partner}, device_id_type=MESH)
    pl.semaphore_wait(barrier, 3 + len(sides))
    step = own_ref.shape[0] // PIECES
    half = PIECES // 2

    def slot(k, m, p):
        rows = pl.ds(p * step, step)
        if k == 0 and m == 0:
            return own_ref.at[rows, :]
        return buf_ref.at[k * across + m - 1, rows, :]

    def send(src, dst, sent, got, axis, where):
        return pltpu.make_async_remote_copy(
            src_ref=src, dst_ref=dst, send_sem=sent, recv_sem=got,
            device_id={axis: where}, device_id_type=MESH,
        )

    def hop(k, p):
        return send(slot(k, 0, p), slot(k + 1, 0, p), zs.at[k, p], zr.at[k, p], "seq", up)

    def swap(k, m, p):
        return send(
            slot(k, 0, p), slot(k, m, p), xs.at[k, m - 1, p], xr.at[k, m - 1, p], "seq", sides[m - 1]
        )

    def relay(m, p):
        return send(slot(0, m, p), slot(1, m, p), rs.at[m - 1, p], rr.at[m - 1, p], "seq", up)

    def cross(g):
        cols = pl.ds(pl.multiple_of((2 * g + 1 - core) * width, HEAD_DIM), width)
        return send(
            w_ref.at[:, cols], w2_ref.at[:, pl.ds(g * width, width)], ws.at[g], wr.at[g], "tensor", partner
        )

    def next_up():
        return send(owns[1], ahead[0], hs.at[0], hr.at[0], "seq", up)

    def next_side(m):
        return send(owns[1], ahead[m], hs.at[m], hr.at[m], "seq", sides[m - 1])

    started = []

    def go(copy):
        copy.start()
        started.append(copy)

    for k in range(along):
        for p in range(PIECES):
            if k:
                hop(k - 1, p).wait_recv()
            if k < along - 1:
                go(hop(k, p))
            if k != 1 or p < half:
                for m in range(1, across):
                    go(swap(k, m, p))
        if k == 0:
            for g in range(groups):
                go(cross(g))
    for p in range(half, PIECES):
        for m in range(1, across):
            swap(0, m, p).wait_recv()
            go(relay(m, p))
    if kvs > 1:
        go(next_up())
        for m in range(1, across):
            go(next_side(m))
    for k in range(along):
        for m in range(1, across):
            for p in range(PIECES):
                if k == 0 and p >= half:
                    continue
                (relay(m, p) if k == 1 and p >= half else swap(k, m, p)).wait_recv()
    for copy in started:
        copy.wait_send()
    for g in range(groups):
        cross(g).wait_recv()
    if kvs > 1:
        next_up().wait_recv()
        for m in range(1, across):
            next_side(m).wait_recv()


def gather(owns, out_weight, along, across, n_tensor):
    groups = n_tensor // 2
    width = out_weight.shape[1] // n_tensor
    owns = owns[:2]
    length = owns[0].shape[0]
    piece = jax.ShapeDtypeStruct((length, HEAD_DIM), owns[0].dtype)
    ahead = [piece] * across if len(owns) > 1 else []
    dma = pltpu.SemaphoreType.DMA
    near = (along, PIECES)
    side = (along, across - 1, PIECES)
    extra = (across - 1, PIECES)
    outs = [
        jax.ShapeDtypeStruct((along * across - 1, length, HEAD_DIM), owns[0].dtype),
        jax.ShapeDtypeStruct((out_weight.shape[0], groups * width), out_weight.dtype),
    ] + ahead
    return pl.pallas_call(
        functools.partial(
            gather_kernel, along=along, across=across, width=width, groups=groups, kvs=len(owns)
        ),
        out_shape=outs,
        in_specs=[pl.BlockSpec(memory_space=pl.ANY)] * (len(owns) + 1),
        out_specs=[pl.BlockSpec(memory_space=pl.ANY)] * len(outs),
        scratch_shapes=[
            dma(near), dma(near), dma(side), dma(side), dma(extra), dma(extra),
            dma((groups,)), dma((groups,)), dma((across,)), dma((across,)),
        ],
        compiler_params=pltpu.CompilerParams(collective_id=0, has_side_effects=True),
        name="gather",
    )(*owns, out_weight)


def attend_kernel(meta_ref, query_ref, *refs, n_shards, kv, first_unit, units, blocks, base, kmax, n_units):
    shards, (o_ref, kv_ref, q_ref, table, sems) = refs[:n_shards], refs[-5:]
    length = shards[0].shape[-2]
    v_rows = length // 2
    flat = []
    for ref in shards:
        if len(ref.shape) == 3:
            flat += [ref.at[i] for i in range(ref.shape[0])]
        else:
            flat.append(ref)
    copies = [
        pltpu.make_async_copy(ref, kv_ref.at[pl.ds(i * length, length), :], sems.at[i])
        for i, ref in enumerate(flat)
    ]
    tokens, width = q_ref.shape
    copies.append(
        pltpu.make_async_copy(
            query_ref.at[pl.ds(base * BLOCK, tokens), pl.ds(kv * width, width)], q_ref, sems.at[len(flat)]
        )
    )
    stride = table.shape[0]
    copies.insert(0, pltpu.make_async_copy(meta_ref.at[pl.ds(kv * stride, stride)], table, sems.at[len(flat) + 1]))
    for copy in copies:
        copy.start()
    for copy in copies:
        copy.wait()
    coef = HEAD_DIM ** (-0.5) * LOG2E
    key_pos = lax.broadcasted_iota(jnp.int32, (BLOCK, BLOCK), 0)
    query_pos = lax.broadcasted_iota(jnp.int32, (BLOCK, BLOCK), 1)
    causal = key_pos <= query_pos

    def run(first, depth):
        sets = []
        for side in range(PAIR):
            unit = table[first + side]
            count = table[n_units + unit]
            head = unit // blocks
            block = unit % blocks - base
            rows = pl.ds(pl.multiple_of(block * BLOCK, BLOCK), BLOCK)
            cols = pl.ds(pl.multiple_of(head * HEAD_DIM, HEAD_DIM), HEAD_DIM)
            at = 2 * n_units + unit * kmax
            own = table[at]
            chosen = [own]
            for slot in range(1, depth):
                chosen.append(jnp.where(slot < count, table[at + slot], own))
            sets.append((count, rows, cols, chosen))
        scored = []
        for count, rows, cols, chosen in sets:
            q = q_ref[rows, cols]
            scores = []
            top = None
            for slot in range(depth):
                start = pl.multiple_of(chosen[slot], BLOCK)
                s = lax.dot_general(
                    kv_ref[pl.ds(start, BLOCK), :], q, (((1,), (1,)), ((), ())),
                    preferred_element_type=jnp.float32,
                )
                if slot == 0:
                    s = jnp.where(causal, s, NEG)
                scores.append(s)
                part = jnp.max(s.reshape(BLOCK // 8, 8, BLOCK), axis=0)
                if slot:
                    part = jnp.where(slot < count, part, NEG)
                top = part if top is None else jnp.maximum(top, part)
            scored.append((scores, jnp.max(top, axis=0, keepdims=True) * coef))
        for (count, rows, cols, chosen), (scores, top) in zip(sets, scored):
            acc = None
            total = None
            for slot in range(0, depth, 2):
                n = min(2, depth - slot)
                tops = [jnp.where(slot + i < count, top, -NEG) if slot + i else top for i in range(n)]
                probs = [jnp.exp2(scores[slot + i] * coef - tops[i]) for i in range(n)]
                for p in probs:
                    part = jnp.sum(p.reshape(BLOCK // 8, 8, BLOCK), axis=0)
                    total = part if total is None else total + part
                vals = [
                    kv_ref[pl.ds(pl.multiple_of(chosen[slot + i] + v_rows, BLOCK), BLOCK), :]
                    for i in range(n)
                ]
                if n == 2:
                    lhs = jnp.concatenate(vals, axis=1)
                    rhs = jnp.concatenate([p.astype(jnp.bfloat16) for p in probs], axis=0)
                else:
                    lhs, rhs = vals[0], probs[0].astype(jnp.bfloat16)
                term = jnp.dot(lhs, rhs, preferred_element_type=jnp.float32)
                acc = term if acc is None else acc + term
            out = acc / jnp.sum(total, axis=0, keepdims=True)
            o_ref[rows, cols] = out.T.astype(jnp.bfloat16)

    def loop(index, carry):
        first = first_unit + index * PAIR
        most = table[n_units + table[first + PAIR - 1]]
        below = 0
        for depth in [d for d in DEPTHS if d < kmax] + [kmax]:

            @pl.when((most > below) & (most <= depth))
            def _(depth=depth):
                run(first, depth)

            below = depth
        return carry

    lax.fori_loop(0, units // PAIR, loop, 0)


def attend(queries, shards, meta, units, kv, base, count, kmax, whole=False, into=None, deps=()):
    blocks = queries.shape[0] // BLOCK
    ratio = units // blocks
    width = ratio * HEAD_DIM
    tokens = count * BLOCK
    n_copies = sum(s.shape[0] if s.ndim == 3 else 1 for s in shards)
    rows = n_copies * shards[0].shape[-2]
    chain = [] if into is None else [into]
    hbm = pl.BlockSpec(memory_space=pl.ANY)
    return pl.pallas_call(
        functools.partial(
            attend_kernel, n_shards=len(shards), kv=kv, first_unit=base * ratio, units=count * ratio,
            blocks=blocks, base=base, kmax=kmax, n_units=units,
        ),
        out_shape=jax.ShapeDtypeStruct((queries.shape[0] if whole else tokens, width), jnp.bfloat16),
        grid=(1,),
        in_specs=[hbm] * (2 + len(shards) + len(chain) + len(deps)),
        out_specs=pl.BlockSpec((tokens, width), lambda i: (base // count if whole else 0, 0)),
        input_output_aliases={2 + len(shards): 0} if chain else {},
        scratch_shapes=[
            pltpu.VMEM((rows, HEAD_DIM), jnp.bfloat16),
            pltpu.VMEM((tokens, width), jnp.bfloat16),
            pltpu.SMEM((meta.shape[0] // (queries.shape[1] // width),), jnp.int32),
            pltpu.SemaphoreType.DMA((n_copies + 2,)),
        ],
        compiler_params=pltpu.CompilerParams(vmem_limit_bytes=VMEM),
        cost_estimate=pl.CostEstimate(
            flops=count * ratio * kmax * 24 * BLOCK**3, bytes_accessed=rows * 2 * HEAD_DIM, transcendentals=0
        ),
        name="attend",
    )(meta, queries, *shards, *chain, *deps)


def away_kernel(*refs, offs, groups, width, tile):
    k = len(offs)
    parts, (w_ref, w2_ref, o_ref), others = refs[:k], refs[k : k + 3], refs[k + 3 : 2 * k + 3]
    mine, theirs, tiles, acc, w_sem, in_sem, sent, got, out_sem = refs[2 * k + 3 :]
    rows = mine.shape[0]
    per = width // tile
    n = (groups - 1) * per
    tensor = lax.axis_index("tensor")
    core = lax.rem(tensor, 2)
    row = tensor // 2
    partner = tensor + 1 - 2 * core
    barrier = pltpu.get_barrier_semaphore()
    pl.semaphore_signal(barrier, inc=1, device_id={"tensor": partner}, device_id_type=MESH)

    def fetch(half, t):
        g = lax.rem(row + 1 + t // per, groups)
        first = (g if half else 2 * g + core) * width + lax.rem(t, per) * tile
        src = w2_ref if half else w_ref
        at = half * n + t
        return pltpu.make_async_copy(
            src.at[:, pl.ds(pl.multiple_of(first, HEAD_DIM), tile)], tiles.at[at], w_sem.at[at]
        )

    def cols(j):
        size = parts[j].shape[1]
        return pl.ds(j * size, size)

    def load(j):
        return pltpu.make_async_copy(parts[j].at[pl.ds(offs[j], rows), :], mine.at[:, cols(j)], in_sem.at[j])

    def pass_on(j):
        return pltpu.make_async_remote_copy(
            src_ref=parts[j].at[pl.ds(offs[j], rows), :], dst_ref=theirs.at[:, cols(j)],
            send_sem=sent.at[j], recv_sem=got.at[j],
            device_id={"tensor": partner}, device_id_type=MESH,
        )

    def keep(j):
        return pltpu.make_async_copy(theirs.at[:, cols(j)], others[j], out_sem.at[j])

    for j in range(k):
        load(j).start()
    for half in range(2):
        for t in range(n):
            fetch(half, t).start()
    pl.semaphore_wait(barrier, 1)
    for j in range(k):
        pass_on(j).start()
    for j in range(k):
        load(j).wait()

    def first(t, carry):
        fetch(0, t).wait()
        acc[t] = jnp.dot(mine[...], tiles[t], preferred_element_type=jnp.float32)
        return carry

    lax.fori_loop(0, n, first, 0)
    for j in range(k):
        pass_on(j).wait_recv()
        keep(j).start()

    def second(t, carry):
        fetch(1, t).wait()
        total = acc[t] + jnp.dot(theirs[...], tiles[n + t], preferred_element_type=jnp.float32)
        at = pl.ds(pl.multiple_of(lax.rem(t, per) * tile, HEAD_DIM), tile)
        o_ref[t // per, :, at] = total.astype(jnp.bfloat16)
        return carry

    lax.fori_loop(0, n, second, 0)
    for j in range(k):
        pass_on(j).wait_send()
        keep(j).wait()


def away(parts, offs, rows, weight, weight2, width, groups, index):
    depth = weight.shape[0]
    tile = min(512, width)
    n = (groups - 1) * (width // tile)
    k = len(parts)
    hbm = pl.BlockSpec(memory_space=pl.ANY)
    dma = pltpu.SemaphoreType.DMA
    outs = [jax.ShapeDtypeStruct((groups - 1, rows, width), jnp.bfloat16)]
    outs += [jax.ShapeDtypeStruct((rows, p.shape[1]), jnp.bfloat16) for p in parts]
    return pl.pallas_call(
        functools.partial(away_kernel, offs=offs, groups=groups, width=width, tile=tile),
        out_shape=outs,
        in_specs=[hbm] * (k + 2),
        out_specs=[pl.BlockSpec(memory_space=pltpu.VMEM)] + [hbm] * k,
        scratch_shapes=[
            pltpu.VMEM((rows, depth), jnp.bfloat16),
            pltpu.VMEM((rows, depth), jnp.bfloat16),
            pltpu.VMEM((2 * n, depth, tile), jnp.bfloat16),
            pltpu.VMEM((n, rows, tile), jnp.float32),
            dma((2 * n,)), dma((k,)), dma((k,)), dma((k,)), dma((k,)),
        ],
        compiler_params=pltpu.CompilerParams(
            collective_id=1 + index, has_side_effects=True, vmem_limit_bytes=VMEM
        ),
        cost_estimate=pl.CostEstimate(
            flops=4 * rows * depth * (groups - 1) * width, bytes_accessed=4 * depth * (groups - 1) * width,
            transcendentals=0,
        ),
        name="away",
    )(*parts, weight, weight2)


def project_kernel(feat_ref, *refs, sizes, adds, dtype):
    per = len(sizes[0])
    lhs = refs[: len(sizes) * per]
    w_ref, w2_ref = refs[len(sizes) * per], refs[len(sizes) * per + 1]
    extra = refs[len(sizes) * per + 2 : -1]
    o_ref = refs[-1]
    at = 0
    for c, widths in enumerate(sizes):
        acc = None
        for half, weights in ((0, w_ref), (1, w2_ref)):
            depth = 0
            for j in range(per // 2):
                ref = lhs[c * per + half * (per // 2) + j]
                term = jnp.dot(
                    ref[...], weights[depth : depth + ref.shape[1], :], preferred_element_type=jnp.float32
                )
                acc = term if acc is None else acc + term
                depth += ref.shape[1]
        rows = lhs[c * per].shape[0]
        for ref in extra[c * adds : (c + 1) * adds]:
            acc = acc + ref[...].astype(jnp.float32)
        out = acc.astype(dtype)
        if len(o_ref.shape) == 3:
            o_ref[0, at : at + rows, :] = out
        else:
            o_ref[at : at + rows, :] = out
        at += rows


def project(chunks, weight, weight2, feats, width, tile, extra=(), full=None, dtype=jnp.bfloat16):
    n = feats.shape[0] // 2
    depth = weight.shape[0]
    tile = min(tile, width)
    per = width // tile
    tokens = sum(chunk[0][2] for chunk in chunks)
    flat = [piece for chunk in chunks for piece in chunk]
    in_specs = [
        pl.BlockSpec((rows, a.shape[1]), lambda g, i, f, b=b: (b, 0)) for a, b, rows in flat
    ]
    in_specs.append(pl.BlockSpec((depth, tile), lambda g, i, f: (0, f[g] * per + i)))
    in_specs.append(pl.BlockSpec((depth, tile), lambda g, i, f: (0, f[n + g] * per + i)))
    for a in extra:
        in_specs.append(pl.BlockSpec((a.shape[0], tile), lambda g, i, f: (0, i)))
    if full is None:
        out_shape = jax.ShapeDtypeStruct((n, tokens, width), dtype)
        out_spec = pl.BlockSpec((1, tokens, tile), lambda g, i, f: (g, 0, i))
    else:
        out_shape = jax.ShapeDtypeStruct((full, width), dtype)
        out_spec = pl.BlockSpec((tokens, tile), lambda g, i, f: (0, i))
    return pl.pallas_call(
        functools.partial(
            project_kernel, sizes=[[p[2] for p in chunk] for chunk in chunks],
            adds=len(extra) // max(1, len(chunks) - 1), dtype=dtype,
        ),
        out_shape=out_shape,
        grid_spec=pltpu.PrefetchScalarGridSpec(
            num_scalar_prefetch=1, grid=(n, per), in_specs=in_specs, out_specs=out_spec,
        ),
        compiler_params=pltpu.CompilerParams(vmem_limit_bytes=VMEM),
        cost_estimate=pl.CostEstimate(
            flops=4 * tokens * depth * n * width, bytes_accessed=4 * depth * n * width, transcendentals=0
        ),
    )(feats, *[a for a, _, _ in flat], weight, weight2, *extra)


def finish_kernel(base_ref, *refs):
    o_ref = refs[-1]
    total = base_ref[...].astype(jnp.float32)
    for ref in refs[:-1]:
        total = total + ref[...].astype(jnp.float32)
    o_ref[...] = total.astype(o_ref.dtype)


def finish(out, terms):
    tokens, width = terms[0].shape
    row = out.shape[0] // tokens - 1
    tile = min(1024, width)
    spec = pl.BlockSpec((tokens, tile), lambda i: (0, i))
    mine = pl.BlockSpec((tokens, tile), lambda i: (row, i))
    return pl.pallas_call(
        finish_kernel,
        out_shape=jax.ShapeDtypeStruct(out.shape, out.dtype),
        grid=(width // tile,),
        in_specs=[mine] + [spec] * len(terms),
        out_specs=mine,
        input_output_aliases={0: 0},
        compiler_params=pltpu.CompilerParams(vmem_limit_bytes=VMEM),
        cost_estimate=pl.CostEstimate(
            flops=tokens * width * 2, bytes_accessed=tokens * width * 6, transcendentals=0
        ),
        name="finish",
    )(out, *terms)


def sizes(blocks, parts):
    quarter = max(1, blocks // parts)
    return [quarter] * (blocks // quarter)


def spans(sizes):
    at = 0
    for size in sizes:
        yield at, size
        at += size


def inner(queries, keys, values, key_blocks, block_counts, out_weight):
    tokens = queries.shape[0]
    n_seq = lax.axis_size("seq")
    n_tensor = lax.axis_size("tensor")
    seq_index = lax.axis_index("seq")
    tensor_index = lax.axis_index("tensor")
    kv_local = keys.shape[1] // HEAD_DIM
    blocks = tokens // BLOCK
    heads, _, kmax = key_blocks.shape
    ratio = heads // kv_local
    last = kv_local - 1
    across = 1
    while across * across * 4 <= n_seq:
        across *= 2
    along = n_seq // across

    value_t = values.reshape(blocks, BLOCK, kv_local, HEAD_DIM).transpose(2, 0, 3, 1)
    owns = [
        jnp.concatenate(
            [keys[:, kv * HEAD_DIM : (kv + 1) * HEAD_DIM], value_t[kv].reshape(tokens, HEAD_DIM)], 0
        )
        for kv in range(kv_local)
    ]

    slots = lax.dynamic_slice_in_dim(key_blocks, seq_index * blocks, blocks, 1)
    counts = lax.dynamic_slice_in_dim(block_counts, seq_index * blocks, blocks, 1)
    shard = slots // blocks
    back_z = (seq_index // across - shard // across + along) % along
    back_x = (seq_index % across - shard % across + across) % across
    starts = ((back_z * across + back_x) * 2 * blocks + slots % blocks) * BLOCK
    counts = counts.reshape(kv_local, ratio * blocks)
    starts = starts.reshape(kv_local, ratio * blocks * kmax)
    chunk_of = []
    for kv in range(kv_local):
        ids = []
        for i, (_, size) in enumerate(spans(sizes(blocks, LATE if kv == last else EARLY))):
            ids += [i] * size
        chunk_of.append(ids)
    key = jnp.asarray(chunk_of, jnp.int32)[:, None, :] * (2 * kmax)
    key = jnp.broadcast_to(key, (kv_local, ratio, blocks)).reshape(kv_local, ratio * blocks)
    order = jnp.argsort(key + counts, axis=1).astype(jnp.int32)

    units = ratio * blocks
    meta = jnp.concatenate([order, counts, starts], axis=1)
    stride = -(-meta.shape[1] // 1024) * 1024
    meta = jnp.pad(meta, ((0, 0), (0, stride - meta.shape[1]))).reshape(-1)

    buf, weight2, *ahead = gather(owns, out_weight, along, across, n_tensor)

    ring = [
        (z * across + x, (z + 1) % along * across + x) for z in range(along) for x in range(across)
    ]
    swaps = [
        [(z * across + x, z * across + (x + shift) % across) for z in range(along) for x in range(across)]
        for shift in range(1, across)
    ]
    gathered = [[owns[0], buf]]
    for kv in range(1, kv_local):
        shards = [owns[kv]]
        if kv == 1:
            held = ahead[0]
            shards += ahead[1:]
        else:
            raise NotImplementedError
        for k in range(1, along):
            shards.append(held)
            mine = held
            if k < along - 1:
                held = lax.ppermute(held, "seq", ring)
            for swap in swaps:
                shards.append(lax.ppermute(mine, "seq", swap))
        gathered.append(shards)

    def attended(kv, base, size, whole=False, into=None, deps=()):
        return attend(queries, gathered[kv], meta, units, kv, base, size, kmax, whole, into, deps)

    whole = []
    deps = ()
    for kv in range(last):
        part = None
        for base, size in spans(sizes(blocks, EARLY)):
            part = attended(kv, base, size, True, part, deps if part is None else ())
        whole.append(part)
        deps = (part,)

    width = out_weight.shape[1] // n_tensor
    rows_y = n_tensor // 2
    feats_mine = jnp.stack([tensor_index, tensor_index // 2]).astype(jnp.int32)
    final = list(spans(sizes(blocks, LATE)))
    terms = []
    lhs = []
    for i, (base, size) in enumerate(final):
        part = attended(last, base, size, deps=deps)
        rows = size * BLOCK
        parts = whole + [part]
        offs = [base * BLOCK] * last + [0]
        sums, *others = away(parts, offs, rows, out_weight, weight2, width, rows_y, i)
        got = []
        for k in range(1, rows_y):
            there = [(t, (t + 2 * k) % n_tensor) for t in range(n_tensor)]
            got.append(lax.ppermute(sums[k - 1], "tensor", there))
        terms.append(got)
        lhs.append([(p, o // rows, rows) for p, o in zip(parts, offs)] + [(p, 0, rows) for p in others])
        deps = (sums,)
    out = project(
        lhs, out_weight, weight2, feats_mine, width, 512,
        extra=[t for got in terms[:-1] for t in got], full=tokens,
    )
    return finish(out, terms[-1])


def solution(mesh):
    placed = (
        P("seq", "tensor"),
        P("seq", "tensor"),
        P("seq", "tensor"),
        P("tensor", None, None),
        P("tensor", None),
        P("tensor", None),
    )
    return jax.shard_map(inner, mesh=mesh, in_specs=placed, out_specs=P("seq", "tensor"), check_vma=False)
```

```python
import functools

import jax
import jax.numpy as jnp
from jax import lax
from jax.experimental import pallas as pl
from jax.experimental.pallas import tpu as pltpu
from jax.sharding import PartitionSpec as P


HEAD_DIM = 128
BLOCK = 128
LOG2E = 1.4426950408889634
NEG = -1e30
PAIR = 2
DEPTHS = (2, 4, 6, 8, 12)
PIECES = 8
LATE = 4
AHEAD = 2
VMEM = 62 << 20
MESH = pl.DeviceIdType.MESH


def gather_kernel(*refs, along, across, width, groups, kvs):
    owns, w_ref = refs[:kvs], refs[kvs]
    buf_ref, w2_ref = refs[kvs + 1], refs[kvs + 2]
    n_ahead = across if kvs > 1 else 0
    ahead = refs[kvs + 3 : kvs + 3 + n_ahead]
    zs, zr, xs, xr, rs, rr, ws, wr, hs, hr = refs[kvs + 3 + n_ahead :]
    own_ref = owns[0]
    seq = lax.axis_index("seq")
    z = seq // across
    x = lax.rem(seq, across)
    up = lax.rem(z + 1, along) * across + x
    down = lax.rem(z + along - 1, along) * across + x
    sides = [z * across + lax.rem(x + m, across) for m in range(1, across)]
    core = lax.rem(lax.axis_index("tensor"), 2)
    partner = lax.axis_index("tensor") + 1 - 2 * core
    barrier = pltpu.get_barrier_semaphore()
    for other in [up, down] + sides:
        pl.semaphore_signal(barrier, inc=1, device_id={"seq": other}, device_id_type=MESH)
    pl.semaphore_signal(barrier, inc=1, device_id={"tensor": partner}, device_id_type=MESH)
    pl.semaphore_wait(barrier, 3 + len(sides))
    step = own_ref.shape[0] // PIECES
    half = PIECES // 2

    def slot(k, m, p):
        rows = pl.ds(p * step, step)
        if k == 0 and m == 0:
            return own_ref.at[rows, :]
        return buf_ref.at[k * across + m - 1, rows, :]

    def send(src, dst, sent, got, axis, where):
        return pltpu.make_async_remote_copy(
            src_ref=src, dst_ref=dst, send_sem=sent, recv_sem=got,
            device_id={axis: where}, device_id_type=MESH,
        )

    def hop(k, p):
        return send(slot(k, 0, p), slot(k + 1, 0, p), zs.at[k, p], zr.at[k, p], "seq", up)

    def swap(k, m, p):
        return send(
            slot(k, 0, p), slot(k, m, p), xs.at[k, m - 1, p], xr.at[k, m - 1, p], "seq", sides[m - 1]
        )

    def relay(m, p):
        return send(slot(0, m, p), slot(1, m, p), rs.at[m - 1, p], rr.at[m - 1, p], "seq", up)

    def cross(g):
        cols = pl.ds(pl.multiple_of((2 * g + 1 - core) * width, HEAD_DIM), width)
        return send(
            w_ref.at[:, cols], w2_ref.at[:, pl.ds(g * width, width)], ws.at[g], wr.at[g], "tensor", partner
        )

    def next_up():
        return send(owns[1], ahead[0], hs.at[0], hr.at[0], "seq", up)

    def next_side(m):
        return send(owns[1], ahead[m], hs.at[m], hr.at[m], "seq", sides[m - 1])

    started = []

    def go(copy):
        copy.start()
        started.append(copy)

    for k in range(along):
        for p in range(PIECES):
            if k:
                hop(k - 1, p).wait_recv()
            if k < along - 1:
                go(hop(k, p))
            if k != 1 or p < half:
                for m in range(1, across):
                    go(swap(k, m, p))
        if k == 0:
            for g in range(groups):
                go(cross(g))
    for p in range(half, PIECES):
        for m in range(1, across):
            swap(0, m, p).wait_recv()
            go(relay(m, p))
    if kvs > 1:
        go(next_up())
        for m in range(1, across):
            go(next_side(m))
    for k in range(along):
        for m in range(1, across):
            for p in range(PIECES):
                if k == 0 and p >= half:
                    continue
                (relay(m, p) if k == 1 and p >= half else swap(k, m, p)).wait_recv()
    for copy in started:
        copy.wait_send()
    for g in range(groups):
        cross(g).wait_recv()
    if kvs > 1:
        next_up().wait_recv()
        for m in range(1, across):
            next_side(m).wait_recv()


def gather(owns, out_weight, along, across, n_tensor):
    groups = n_tensor // 2
    width = out_weight.shape[1] // n_tensor
    owns = owns[:2]
    length = owns[0].shape[0]
    piece = jax.ShapeDtypeStruct((length, HEAD_DIM), owns[0].dtype)
    ahead = [piece] * across if len(owns) > 1 else []
    dma = pltpu.SemaphoreType.DMA
    near = (along, PIECES)
    side = (along, across - 1, PIECES)
    extra = (across - 1, PIECES)
    outs = [
        jax.ShapeDtypeStruct((along * across - 1, length, HEAD_DIM), owns[0].dtype),
        jax.ShapeDtypeStruct((out_weight.shape[0], groups * width), out_weight.dtype),
    ] + ahead
    return pl.pallas_call(
        functools.partial(
            gather_kernel, along=along, across=across, width=width, groups=groups, kvs=len(owns)
        ),
        out_shape=outs,
        in_specs=[pl.BlockSpec(memory_space=pl.ANY)] * (len(owns) + 1),
        out_specs=[pl.BlockSpec(memory_space=pl.ANY)] * len(outs),
        scratch_shapes=[
            dma(near), dma(near), dma(side), dma(side), dma(extra), dma(extra),
            dma((groups,)), dma((groups,)), dma((across,)), dma((across,)),
        ],
        compiler_params=pltpu.CompilerParams(collective_id=0, has_side_effects=True),
        name="gather",
    )(*owns, out_weight)


def attend_kernel(meta_ref, query_ref, *refs, n_shards, kv, first_unit, units, blocks, base, kmax, n_units):
    shards, (o_ref, kv_ref, q_ref, table, sems) = refs[:n_shards], refs[-5:]
    length = shards[0].shape[-2]
    v_rows = length // 2
    flat = []
    for ref in shards:
        if len(ref.shape) == 3:
            flat += [ref.at[i] for i in range(ref.shape[0])]
        else:
            flat.append(ref)
    copies = [
        pltpu.make_async_copy(ref, kv_ref.at[pl.ds(i * length, length), :], sems.at[i])
        for i, ref in enumerate(flat)
    ]
    tokens, width = q_ref.shape
    copies.append(
        pltpu.make_async_copy(
            query_ref.at[pl.ds(base * BLOCK, tokens), pl.ds(kv * width, width)], q_ref, sems.at[len(flat)]
        )
    )
    stride = table.shape[0]
    copies.insert(0, pltpu.make_async_copy(meta_ref.at[pl.ds(kv * stride, stride)], table, sems.at[len(flat) + 1]))
    for copy in copies:
        copy.start()
    for copy in copies:
        copy.wait()
    coef = HEAD_DIM ** (-0.5) * LOG2E
    key_pos = lax.broadcasted_iota(jnp.int32, (BLOCK, BLOCK), 0)
    query_pos = lax.broadcasted_iota(jnp.int32, (BLOCK, BLOCK), 1)
    causal = key_pos <= query_pos

    def run(first, depth):
        sets = []
        for side in range(PAIR):
            unit = table[first + side]
            count = table[n_units + unit]
            head = unit // blocks
            block = unit % blocks - base
            rows = pl.ds(pl.multiple_of(block * BLOCK, BLOCK), BLOCK)
            cols = pl.ds(pl.multiple_of(head * HEAD_DIM, HEAD_DIM), HEAD_DIM)
            at = 2 * n_units + unit * kmax
            own = table[at]
            chosen = [own]
            for slot in range(1, depth):
                chosen.append(jnp.where(slot < count, table[at + slot], own))
            sets.append((count, rows, cols, chosen))
        scored = []
        for count, rows, cols, chosen in sets:
            q = q_ref[rows, cols]
            scores = []
            top = None
            for slot in range(depth):
                start = pl.multiple_of(chosen[slot], BLOCK)
                s = lax.dot_general(
                    kv_ref[pl.ds(start, BLOCK), :], q, (((1,), (1,)), ((), ())),
                    preferred_element_type=jnp.float32,
                )
                if slot == 0:
                    s = jnp.where(causal, s, NEG)
                scores.append(s)
                part = jnp.max(s.reshape(BLOCK // 8, 8, BLOCK), axis=0)
                if slot:
                    part = jnp.where(slot < count, part, NEG)
                top = part if top is None else jnp.maximum(top, part)
            scored.append((scores, jnp.max(top, axis=0, keepdims=True) * coef))
        for (count, rows, cols, chosen), (scores, top) in zip(sets, scored):
            acc = None
            total = None
            for slot in range(0, depth, 2):
                n = min(2, depth - slot)
                tops = [jnp.where(slot + i < count, top, -NEG) if slot + i else top for i in range(n)]
                probs = [jnp.exp2(scores[slot + i] * coef - tops[i]) for i in range(n)]
                for p in probs:
                    part = jnp.sum(p.reshape(BLOCK // 8, 8, BLOCK), axis=0)
                    total = part if total is None else total + part
                vals = [
                    kv_ref[pl.ds(pl.multiple_of(chosen[slot + i] + v_rows, BLOCK), BLOCK), :]
                    for i in range(n)
                ]
                if n == 2:
                    lhs = jnp.concatenate(vals, axis=1)
                    rhs = jnp.concatenate([p.astype(jnp.bfloat16) for p in probs], axis=0)
                else:
                    lhs, rhs = vals[0], probs[0].astype(jnp.bfloat16)
                term = jnp.dot(lhs, rhs, preferred_element_type=jnp.float32)
                acc = term if acc is None else acc + term
            out = acc / jnp.sum(total, axis=0, keepdims=True)
            o_ref[rows, cols] = out.T.astype(jnp.bfloat16)

    def loop(index, carry):
        first = first_unit + index * PAIR
        most = table[n_units + table[first + PAIR - 1]]
        below = 0
        for depth in [d for d in DEPTHS if d < kmax] + [kmax]:

            @pl.when((most > below) & (most <= depth))
            def _(depth=depth):
                run(first, depth)

            below = depth
        return carry

    lax.fori_loop(0, units // PAIR, loop, 0)


def attend(queries, shards, meta, units, kv, base, count, kmax, deps=()):
    blocks = queries.shape[0] // BLOCK
    ratio = units // blocks
    width = ratio * HEAD_DIM
    tokens = count * BLOCK
    n_copies = sum(s.shape[0] if s.ndim == 3 else 1 for s in shards)
    rows = n_copies * shards[0].shape[-2]
    hbm = pl.BlockSpec(memory_space=pl.ANY)
    return pl.pallas_call(
        functools.partial(
            attend_kernel, n_shards=len(shards), kv=kv, first_unit=base * ratio, units=count * ratio,
            blocks=blocks, base=base, kmax=kmax, n_units=units,
        ),
        out_shape=jax.ShapeDtypeStruct((tokens, width), jnp.bfloat16),
        grid=(1,),
        in_specs=[hbm] * (2 + len(shards) + len(deps)),
        out_specs=pl.BlockSpec((tokens, width), lambda i: (0, 0)),
        scratch_shapes=[
            pltpu.VMEM((rows, HEAD_DIM), jnp.bfloat16),
            pltpu.VMEM((tokens, width), jnp.bfloat16),
            pltpu.SMEM((meta.shape[0] // (queries.shape[1] // width),), jnp.int32),
            pltpu.SemaphoreType.DMA((n_copies + 2,)),
        ],
        compiler_params=pltpu.CompilerParams(vmem_limit_bytes=VMEM),
        cost_estimate=pl.CostEstimate(
            flops=count * ratio * kmax * 24 * BLOCK**3, bytes_accessed=rows * 2 * HEAD_DIM, transcendentals=0
        ),
        name="attend",
    )(meta, queries, *shards, *deps)


def away_kernel(*refs, k, groups, width, tile):
    parts, (w_ref, w2_ref, o_ref), others = refs[:k], refs[k : k + 3], refs[k + 3 : 2 * k + 3]
    mine, theirs, tiles, acc, w_sem, in_sem, sent, got, out_sem = refs[2 * k + 3 :]
    per = width // tile
    n = (groups - 1) * per
    tensor = lax.axis_index("tensor")
    core = lax.rem(tensor, 2)
    row = tensor // 2
    partner = tensor + 1 - 2 * core
    barrier = pltpu.get_barrier_semaphore()
    pl.semaphore_signal(barrier, inc=1, device_id={"tensor": partner}, device_id_type=MESH)

    def fetch(half, t):
        g = lax.rem(row + 1 + t // per, groups)
        first = (g if half else 2 * g + core) * width + lax.rem(t, per) * tile
        src = w2_ref if half else w_ref
        at = half * n + t
        return pltpu.make_async_copy(
            src.at[:, pl.ds(pl.multiple_of(first, HEAD_DIM), tile)], tiles.at[at], w_sem.at[at]
        )

    def cols(j):
        size = parts[j].shape[1]
        return pl.ds(j * size, size)

    def load(j):
        return pltpu.make_async_copy(parts[j], mine.at[:, cols(j)], in_sem.at[j])

    def pass_on(j):
        return pltpu.make_async_remote_copy(
            src_ref=parts[j], dst_ref=theirs.at[:, cols(j)],
            send_sem=sent.at[j], recv_sem=got.at[j],
            device_id={"tensor": partner}, device_id_type=MESH,
        )

    def keep(j):
        return pltpu.make_async_copy(theirs.at[:, cols(j)], others[j], out_sem.at[j])

    for j in range(k):
        load(j).start()
    for t in range(min(AHEAD, n)):
        fetch(0, t).start()
    pl.semaphore_wait(barrier, 1)
    for j in range(k):
        pass_on(j).start()
    for j in range(k):
        load(j).wait()

    def first(t, carry):
        fetch(0, t).wait()

        @pl.when(t + AHEAD < n)
        def _():
            fetch(0, t + AHEAD).start()

        @pl.when(t + AHEAD >= n)
        def _():
            fetch(1, t + AHEAD - n).start()

        acc[t] = jnp.dot(mine[...], tiles[t], preferred_element_type=jnp.float32)
        return carry

    lax.fori_loop(0, n, first, 0)
    for j in range(k):
        pass_on(j).wait_recv()
        keep(j).start()

    def second(t, carry):
        fetch(1, t).wait()

        @pl.when(t + AHEAD < n)
        def _():
            fetch(1, t + AHEAD).start()

        total = acc[t] + jnp.dot(theirs[...], tiles[n + t], preferred_element_type=jnp.float32)
        at = pl.ds(pl.multiple_of(lax.rem(t, per) * tile, HEAD_DIM), tile)
        o_ref[t // per, :, at] = total.astype(jnp.bfloat16)
        return carry

    lax.fori_loop(0, n, second, 0)
    for j in range(k):
        pass_on(j).wait_send()
        keep(j).wait()


def away(parts, rows, weight, weight2, width, groups, index):
    depth = weight.shape[0]
    tile = min(512, width)
    n = (groups - 1) * (width // tile)
    k = len(parts)
    hbm = pl.BlockSpec(memory_space=pl.ANY)
    dma = pltpu.SemaphoreType.DMA
    outs = [jax.ShapeDtypeStruct((groups - 1, rows, width), jnp.bfloat16)]
    outs += [jax.ShapeDtypeStruct((rows, p.shape[1]), jnp.bfloat16) for p in parts]
    return pl.pallas_call(
        functools.partial(away_kernel, k=len(parts), groups=groups, width=width, tile=tile),
        out_shape=outs,
        in_specs=[hbm] * (k + 2),
        out_specs=[pl.BlockSpec(memory_space=pltpu.VMEM)] + [hbm] * k,
        scratch_shapes=[
            pltpu.VMEM((rows, depth), jnp.bfloat16),
            pltpu.VMEM((rows, depth), jnp.bfloat16),
            pltpu.VMEM((2 * n, depth, tile), jnp.bfloat16),
            pltpu.VMEM((n, rows, tile), jnp.float32),
            dma((2 * n,)), dma((k,)), dma((k,)), dma((k,)), dma((k,)),
        ],
        compiler_params=pltpu.CompilerParams(
            collective_id=1 + index, has_side_effects=True, vmem_limit_bytes=VMEM
        ),
        cost_estimate=pl.CostEstimate(
            flops=4 * rows * depth * (groups - 1) * width, bytes_accessed=4 * depth * (groups - 1) * width,
            transcendentals=0,
        ),
        name="away",
    )(*parts, weight, weight2)


def project_kernel(feat_ref, *refs, sizes, adds, dtype):
    per = len(sizes[0])
    lhs = refs[: len(sizes) * per]
    w_ref, w2_ref = refs[len(sizes) * per], refs[len(sizes) * per + 1]
    extra = refs[len(sizes) * per + 2 : -1]
    o_ref = refs[-1]
    at = 0
    for c, widths in enumerate(sizes):
        acc = None
        for half, weights in ((0, w_ref), (1, w2_ref)):
            depth = 0
            for j in range(per // 2):
                ref = lhs[c * per + half * (per // 2) + j]
                term = jnp.dot(
                    ref[...], weights[depth : depth + ref.shape[1], :], preferred_element_type=jnp.float32
                )
                acc = term if acc is None else acc + term
                depth += ref.shape[1]
        rows = lhs[c * per].shape[0]
        for ref in extra[c * adds : (c + 1) * adds]:
            acc = acc + ref[...].astype(jnp.float32)
        out = acc.astype(dtype)
        if len(o_ref.shape) == 3:
            o_ref[0, at : at + rows, :] = out
        else:
            o_ref[at : at + rows, :] = out
        at += rows


def project(chunks, weight, weight2, feats, width, tile, extra=(), full=None, dtype=jnp.bfloat16):
    n = feats.shape[0] // 2
    depth = weight.shape[0]
    tile = min(tile, width)
    per = width // tile
    tokens = sum(chunk[0][2] for chunk in chunks)
    flat = [piece for chunk in chunks for piece in chunk]
    in_specs = [
        pl.BlockSpec((rows, a.shape[1]), lambda g, i, f, b=b: (b, 0)) for a, b, rows in flat
    ]
    in_specs.append(pl.BlockSpec((depth, tile), lambda g, i, f: (0, f[g] * per + i)))
    in_specs.append(pl.BlockSpec((depth, tile), lambda g, i, f: (0, f[n + g] * per + i)))
    for a in extra:
        in_specs.append(pl.BlockSpec((a.shape[0], tile), lambda g, i, f: (0, i)))
    if full is None:
        out_shape = jax.ShapeDtypeStruct((n, tokens, width), dtype)
        out_spec = pl.BlockSpec((1, tokens, tile), lambda g, i, f: (g, 0, i))
    else:
        out_shape = jax.ShapeDtypeStruct((full, width), dtype)
        out_spec = pl.BlockSpec((tokens, tile), lambda g, i, f: (0, i))
    return pl.pallas_call(
        functools.partial(
            project_kernel, sizes=[[p[2] for p in chunk] for chunk in chunks],
            adds=len(extra) // max(1, len(chunks) - 1), dtype=dtype,
        ),
        out_shape=out_shape,
        grid_spec=pltpu.PrefetchScalarGridSpec(
            num_scalar_prefetch=1, grid=(n, per), in_specs=in_specs, out_specs=out_spec,
        ),
        compiler_params=pltpu.CompilerParams(vmem_limit_bytes=VMEM),
        cost_estimate=pl.CostEstimate(
            flops=4 * tokens * depth * n * width, bytes_accessed=4 * depth * n * width, transcendentals=0
        ),
    )(feats, *[a for a, _, _ in flat], weight, weight2, *extra)


def finish_kernel(base_ref, *refs):
    o_ref = refs[-1]
    total = base_ref[...].astype(jnp.float32)
    for ref in refs[:-1]:
        total = total + ref[...].astype(jnp.float32)
    o_ref[...] = total.astype(o_ref.dtype)


def finish(out, terms):
    tokens, width = terms[0].shape
    row = out.shape[0] // tokens - 1
    tile = min(1024, width)
    spec = pl.BlockSpec((tokens, tile), lambda i: (0, i))
    mine = pl.BlockSpec((tokens, tile), lambda i: (row, i))
    return pl.pallas_call(
        finish_kernel,
        out_shape=jax.ShapeDtypeStruct(out.shape, out.dtype),
        grid=(width // tile,),
        in_specs=[mine] + [spec] * len(terms),
        out_specs=mine,
        input_output_aliases={0: 0},
        compiler_params=pltpu.CompilerParams(vmem_limit_bytes=VMEM),
        cost_estimate=pl.CostEstimate(
            flops=tokens * width * 2, bytes_accessed=tokens * width * 6, transcendentals=0
        ),
        name="finish",
    )(out, *terms)


def sizes(blocks, parts):
    quarter = max(1, blocks // parts)
    return [quarter] * (blocks // quarter)


def spans(sizes):
    at = 0
    for size in sizes:
        yield at, size
        at += size


def inner(queries, keys, values, key_blocks, block_counts, out_weight):
    tokens = queries.shape[0]
    n_seq = lax.axis_size("seq")
    n_tensor = lax.axis_size("tensor")
    seq_index = lax.axis_index("seq")
    tensor_index = lax.axis_index("tensor")
    kv_local = keys.shape[1] // HEAD_DIM
    blocks = tokens // BLOCK
    heads, _, kmax = key_blocks.shape
    ratio = heads // kv_local
    last = kv_local - 1
    across = 1
    while across * across * 4 <= n_seq:
        across *= 2
    along = n_seq // across

    value_t = values.reshape(blocks, BLOCK, kv_local, HEAD_DIM).transpose(2, 0, 3, 1)
    owns = [
        jnp.concatenate(
            [keys[:, kv * HEAD_DIM : (kv + 1) * HEAD_DIM], value_t[kv].reshape(tokens, HEAD_DIM)], 0
        )
        for kv in range(kv_local)
    ]

    slots = lax.dynamic_slice_in_dim(key_blocks, seq_index * blocks, blocks, 1)
    counts = lax.dynamic_slice_in_dim(block_counts, seq_index * blocks, blocks, 1)
    shard = slots // blocks
    back_z = (seq_index // across - shard // across + along) % along
    back_x = (seq_index % across - shard % across + across) % across
    starts = ((back_z * across + back_x) * 2 * blocks + slots % blocks) * BLOCK
    counts = counts.reshape(kv_local, ratio * blocks)
    starts = starts.reshape(kv_local, ratio * blocks * kmax)
    chunk_of = []
    for _ in range(kv_local):
        ids = []
        for i, (_, size) in enumerate(spans(sizes(blocks, LATE))):
            ids += [i] * size
        chunk_of.append(ids)
    key = jnp.asarray(chunk_of, jnp.int32)[:, None, :] * (2 * kmax)
    key = jnp.broadcast_to(key, (kv_local, ratio, blocks)).reshape(kv_local, ratio * blocks)
    order = jnp.argsort(key + counts, axis=1).astype(jnp.int32)

    units = ratio * blocks
    meta = jnp.concatenate([order, counts, starts], axis=1)
    stride = -(-meta.shape[1] // 1024) * 1024
    meta = jnp.pad(meta, ((0, 0), (0, stride - meta.shape[1]))).reshape(-1)

    buf, weight2, *ahead = gather(owns, out_weight, along, across, n_tensor)

    ring = [
        (z * across + x, (z + 1) % along * across + x) for z in range(along) for x in range(across)
    ]
    swaps = [
        [(z * across + x, z * across + (x + shift) % across) for z in range(along) for x in range(across)]
        for shift in range(1, across)
    ]
    gathered = [[owns[0], buf]]
    for kv in range(1, kv_local):
        shards = [owns[kv]]
        if kv == 1:
            held = ahead[0]
            shards += ahead[1:]
        else:
            raise NotImplementedError
        for k in range(1, along):
            shards.append(held)
            mine = held
            if k < along - 1:
                held = lax.ppermute(held, "seq", ring)
            for swap in swaps:
                shards.append(lax.ppermute(mine, "seq", swap))
        gathered.append(shards)

    def attended(kv, base, size, deps=()):
        return attend(queries, gathered[kv], meta, units, kv, base, size, kmax, deps)

    final = list(spans(sizes(blocks, LATE)))
    early = {}
    deps = ()

    def attended_early(i, deps):
        for kv in range(last):
            early[kv, i] = attended(kv, *final[i], deps=deps)
            deps = (early[kv, i],)
        return deps

    for i in range(len(final) - 1):
        deps = attended_early(i, deps)

    width = out_weight.shape[1] // n_tensor
    rows_y = n_tensor // 2
    feats_mine = jnp.stack([tensor_index, tensor_index // 2]).astype(jnp.int32)
    terms = []
    lhs = []
    for i, (base, size) in enumerate(final):
        if i == len(final) - 1:
            deps = attended_early(i, deps)
        rows = size * BLOCK
        parts = [early[kv, i] for kv in range(last)] + [attended(last, base, size, deps=deps)]
        sums, *others = away(parts, rows, out_weight, weight2, width, rows_y, i)
        got = []
        for k in range(1, rows_y):
            there = [(t, (t + 2 * k) % n_tensor) for t in range(n_tensor)]
            got.append(lax.ppermute(sums[k - 1], "tensor", there))
        terms.append(got)
        lhs.append([(p, 0, rows) for p in parts + others])
        deps = (sums,)
    out = project(
        lhs, out_weight, weight2, feats_mine, width, 512,
        extra=[t for got in terms[:-1] for t in got], full=tokens,
    )
    return finish(out, terms[-1])


def solution(mesh):
    placed = (
        P("seq", "tensor"),
        P("seq", "tensor"),
        P("seq", "tensor"),
        P("tensor", None, None),
        P("tensor", None),
        P("tensor", None),
    )
    return jax.shard_map(inner, mesh=mesh, in_specs=placed, out_specs=P("seq", "tensor"), check_vma=False)
```
